32 devices in a mesh: grp: 1, wide: 8 (over z, y), narrow: 4 (over x, core).
Axes of the slice: x: 2, y: 2, z: 4, core: 2. Of those that a mesh axis runs over, the one named last changes fastest.
Arguments:
- vectors: bfloat16 [512, 2, 3, 16, 512], P('grp', None, None, 'wide', 'narrow'), may hold values from -6 to 6
- links: float32 [3, 2, 3, 3, 16, 512], P('grp', None, None, None, 'wide', 'narrow'), may hold values from -4 to 4
- directions: int32 [3], replicated, may hold values from 0 to 2, each once
- peram: bfloat16 [2, 512, 256], P('grp', 'wide', 'narrow'), may hold values from -0.1875 to 0.1875
Outputs:
- elementals: float32 [3, 2, 512, 512], P('grp', None, 'wide')
- products: float32 [3, 2, 512, 256], P('grp', None, 'wide', 'narrow')
The draws below stay inside these ranges and needn't reach their ends.
All inputs are finite; a program needn't handle non-finite values.
Results may differ from the reference program's by a relative error of at most 0.004.
Values may be sent and summed in bfloat16 or wider, within the bound.
A program may use at most 64 MiB of HBM per device.

```python
import math
import jax
import jax.numpy as jnp
from jax import lax

NVEC = 512
NCOL = 256
NDIR = 3
NX = 16
NY = 32
NZ = 16


def level_of(key, dims, pieces, least, largest):
    gain = 1.0
    for dim, parts in pieces:
        draws = jax.random.uniform(jax.random.fold_in(jax.random.fold_in(key, 6), dim), (parts,), jnp.float32, least / len(pieces), largest / len(pieces))
        gain = gain * jnp.repeat(jnp.exp(draws), dims[dim] // parts).reshape((-1,) + (1,) * (len(dims) - 1 - dim))
    return gain


def centred(key, dims, deviation, bound, shards=(), held_as=jnp.bfloat16):
    result = deviation * jax.random.normal(key, dims, jnp.float32)
    if shards:
        result = result * level_of(key, dims, shards, -0.22, 0.18)
    return jnp.clip(result, -bound, bound).astype(held_as)


def setup_inputs(seed: int = 0, part: int = 0) -> dict:
    streams_of = jax.random.split(jax.random.key(seed), 5)
    part_keys = jax.random.split(jax.random.fold_in(streams_of[4], part), 5)
    return {
        "vectors": centred(part_keys[0], (NVEC, 2, 3, NX, NY * NZ), 1.0, 6.0, ((3, 8), (4, 4))),
        "links": centred(part_keys[1], (3, 2, 3, 3, NX, NY * NZ), 0.577, 4.0, ((4, 8), (5, 4)), jnp.float32),
        "directions": jax.random.permutation(streams_of[2], NDIR).astype(jnp.int32),
        "peram": centred(part_keys[3], (2, NVEC, NCOL), (2 * NVEC) ** -0.5, 0.1875, ((1, 8), (2, 4))),
    }


def covariant_product(link_field, shifted):
    link_real = link_field[0][None]
    link_imag = link_field[1][None]
    vec_real = shifted[:, 0][:, None]
    vec_imag = shifted[:, 1][:, None]
    out_real = lax.optimization_barrier(jnp.sum(link_real * vec_real - link_imag * vec_imag, axis=2))
    out_imag = lax.optimization_barrier(jnp.sum(link_real * vec_imag + link_imag * vec_real, axis=2))
    return jnp.stack([out_real, out_imag], 1).astype(jnp.bfloat16)

def reference(vectors, links, directions, peram):
    vec_count = vectors.shape[0]
    col_count = peram.shape[2]
    norm_factor = 1.0 / math.sqrt(12.0 * NX * NY * NZ)

    def plane_step(carry, position):
        plane = lax.dynamic_index_in_dim(vectors, position, 3, keepdims=False)
        ahead = lax.dynamic_index_in_dim(vectors, (position + 1) % NX, 3, keepdims=False)
        link_plane = lax.dynamic_index_in_dim(links, position, 4, keepdims=False)
        along_second = jnp.roll(plane, -NZ, axis=3)
        along_third = jnp.roll(plane.reshape(vec_count, 2, 3, NY, NZ), -1, axis=4).reshape(plane.shape)
        rotated = jnp.concatenate([-plane[:, 1:2], plane[:, 0:1]], 1)
        left_block = jnp.concatenate([plane.reshape(vec_count, -1), rotated.reshape(vec_count, -1)], 0)
        partials = []
        for slot_index in range(NDIR):
            chosen = directions[slot_index]
            shifted = jnp.where(chosen == 0, ahead, jnp.where(chosen == 1, along_second, along_third))
            link_field = jnp.where(chosen == 0, link_plane[0], jnp.where(chosen == 1, link_plane[1], link_plane[2]))
            product = covariant_product(link_field, shifted).reshape(vec_count, -1)
            partials.append(jnp.dot(left_block, product.T, preferred_element_type=jnp.float32))
        return (carry + jnp.stack(partials), None)
    initial = jnp.zeros((NDIR, 2 * vec_count, vec_count), jnp.float32)
    total, _ = lax.scan(plane_step, initial, jnp.arange(NX, dtype=jnp.int32))
    halves = total.reshape(NDIR, 2, vec_count, vec_count) * norm_factor
    real_part = halves[:, 0]
    imag_part = halves[:, 1]
    elementals = jnp.stack([real_part - jnp.swapaxes(real_part, 1, 2), imag_part + jnp.swapaxes(imag_part, 1, 2)], 1)
    elem_low = elementals.astype(jnp.bfloat16)
    left_rows = jnp.concatenate([elem_low[:, 0], elem_low[:, 1]], 2).reshape(NDIR * vec_count, 2 * vec_count)
    peram_real = peram[0]
    peram_imag = peram[1]
    right_block = jnp.concatenate([jnp.concatenate([peram_real, peram_imag], 1), jnp.concatenate([-peram_imag, peram_real], 1)], 0)
    summed = jnp.dot(left_rows, right_block, preferred_element_type=jnp.float32)
    products = summed.reshape(NDIR, vec_count, 2, col_count).transpose(0, 2, 1, 3)
    return (elementals, products)
```

```python
import functools
import math

import jax
import jax.numpy as jnp
from jax import lax
from jax.experimental import pallas as pl
from jax.experimental.pallas import tpu as pltpu
from jax.sharding import PartitionSpec as P

LZ = 16
BLOCK = 128
INNER = 2
MESH = pl.DeviceIdType.MESH
NT = (((1,), (1,)), ((), ()))


def kernel(wides, narrows, norm, vec, links, dirs, peram, elem_out, prod_out,
           pack, halo0, halo1, vmat, f, half, keep, got_core, part, got_x, got_z, got_d,
           piece, full, low, elems, prods, per_own, per_all, per_two, unmix,
           h_send, h_recv, p_send, p_recv, c_send, c_recv, x_send, x_recv,
           z_send, z_recv, b_send, b_recv, d_send, d_recv):
    planes, comps, _, rows, lanes = vec.shape
    count = wides * rows
    groups = count // BLOCK
    per = rows // groups
    across = narrows // 2
    sub = per // across
    outer = wides // INNER
    cols = peram.shape[2]
    slots = count // (lanes // LZ)
    me_w = lax.axis_index("wide")
    me_n = lax.axis_index("narrow")
    core = lax.rem(me_n, 2)
    me_x = me_n // 2
    me_z = me_w // INNER
    me_y = lax.rem(me_w, INNER)

    def copy(src, dst, send, recv, where):
        return pltpu.make_async_remote_copy(
            src_ref=src, dst_ref=dst, send_sem=send, recv_sem=recv,
            device_id=where, device_id_type=MESH)

    def spot(wide, narrow):
        return {"wide": wide, "narrow": narrow}

    barrier = pltpu.get_barrier_semaphore()
    for a in range(wides):
        for b in range(narrows):
            if a or b:
                pl.semaphore_signal(
                    barrier, inc=1, device_id_type=MESH,
                    device_id=spot(lax.rem(me_w + a, wides), lax.rem(me_n + b, narrows)))

    lane = lax.broadcasted_iota(jnp.int32, (per, lanes), 1)

    def pack_rows(i, carry):
        start = pl.multiple_of(i * per, per)
        for plane in range(planes):
            for comp in range(comps):
                total = jnp.zeros((per, lanes), jnp.float32)
                for group in range(lanes // LZ):
                    first = group * slots
                    value = vec[plane, comp, first // rows, pl.ds(first % rows + start, per), :]
                    value = value.astype(jnp.float32)
                    if group:
                        value = pltpu.roll(value, group * LZ, 1)
                    total = jnp.where(lane // LZ == group, value, total)
                pack[plane, comp, pl.ds(start, per), :] = total.astype(jnp.bfloat16)
        return carry

    lax.fori_loop(0, slots // per, pack_rows, 0)

    def stack(i, carry):
        q = i // wides
        w = lax.rem(i, wides)
        start = pl.multiple_of(q * per, per)
        to = pl.multiple_of(i * per, per)
        for plane in range(planes):
            for comp in range(comps):
                at = (plane * comps + comp) * lanes
                vmat[pl.ds(to, per), at:at + lanes] = vec[plane, comp, w, pl.ds(start, per), :]
        return carry

    lax.fori_loop(0, groups * wides, stack, 0)
    for q in range(groups):
        both = jnp.concatenate([peram[c, q * per:(q + 1) * per, :].astype(jnp.float32) for c in range(2)], 1)
        per_own[q] = both.astype(jnp.bfloat16)

    pl.semaphore_wait(barrier, wides * narrows - 1)
    behind = lax.rem(me_w + wides - 1, wides)
    halo_copies = [
        copy(vec.at[0, :, :, pl.ds(q * per, per), :], halo0.at[q], h_send.at[q], h_recv.at[q],
             spot(behind, me_n))
        for q in range(groups)
    ]
    row_copy = copy(pack, halo1, h_send.at[groups], h_recv.at[groups],
                    spot(me_w, lax.rem(me_n + narrows - 1, narrows)))
    row_copy.start()
    for one in halo_copies:
        one.start()
    per_copies = [
        copy(per_own, per_all.at[:, me_z, me_y], p_send.at[step], p_recv.at[step],
             spot(lax.rem(me_z + step, outer) * INNER + me_y, me_n))
        for step in range(1, outer)
    ]
    for one in per_copies:
        one.start()
    per_all[:, me_z, me_y] = per_own[...]
    per_turn = [
        copy(per_all.at[:, :, me_y], per_all.at[:, :, me_y],
             p_send.at[outer + step - 1], p_recv.at[outer + step - 1],
             spot(me_z * INNER + lax.rem(me_y + step, INNER), me_n))
        for step in range(1, INNER)
    ]

    def shifted(direction, plane, comp, q, w):
        here = pl.ds(q * per, per)
        if direction == 0:
            if plane + 1 < planes:
                return vec[plane + 1, comp, w, here, :].astype(jnp.float32)
            return halo0[q, comp, w].astype(jnp.float32)
        own = vec[plane, comp, w, here, :].astype(jnp.float32)
        if direction == 1:
            start = w * rows + q * per
            group = start // slots
            inside = pl.multiple_of(lax.rem(start, slots), per)
            ahead = halo1[plane, comp, pl.ds(inside, per), :].astype(jnp.float32)
            ahead = pltpu.roll(ahead, lanes - LZ - LZ * group, 1)
            return jnp.where(lane < lanes - LZ, pltpu.roll(own, lanes - LZ, 1), ahead)
        return jnp.where(
            lax.rem(lane, LZ) < LZ - 1, pltpu.roll(own, lanes - 1, 1), pltpu.roll(own, LZ - 1, 1))

    def forward(direction, q, chosen):
        for plane in chosen:
            def chunk(w, carry):
                to = pl.multiple_of(w * per, per)
                values = [shifted(direction, plane, comp, q, w) for comp in range(comps)]
                for a in range(3):
                    real = imag = None
                    for b in range(3):
                        link_r = links[direction, 0, a, b, plane:plane + 1, :]
                        link_i = links[direction, 1, a, b, plane:plane + 1, :]
                        term_r = link_r * values[b] - link_i * values[3 + b]
                        term_i = link_r * values[3 + b] + link_i * values[b]
                        real = term_r if real is None else real + term_r
                        imag = term_i if imag is None else imag + term_i
                    real = real.astype(jnp.bfloat16)
                    imag = imag.astype(jnp.bfloat16)
                    at = (plane * comps + a) * lanes
                    up = at + 3 * lanes
                    f[pl.ds(to, per), at:at + lanes] = real
                    f[pl.ds(to, per), up:up + lanes] = imag
                    f[pl.ds(BLOCK + to, per), at:at + lanes] = imag
                    f[pl.ds(BLOCK + to, per), up:up + lanes] = -real
                return carry

            lax.fori_loop(0, wides, chunk, 0)

    def spread(d, c, b, value):
        keep[d, c, :, :, b] = value.reshape(wides, across, sub, BLOCK)

    def fold(d, q):
        half[q] = lax.dot_general(vmat[...], f[...], NT, preferred_element_type=jnp.float32)
        own = slice(q * BLOCK, (q + 1) * BLOCK)
        for i in range(q + 1):
            top = slice(i * BLOCK, (i + 1) * BLOCK)
            for c in range(2):
                side = slice(c * BLOCK, (c + 1) * BLOCK)
                there = half[q, top, side]
                back = half[i, own, side]
                turned = back.T
                spread(d, c, q * q + i, ((there - turned) if c == 0 else (there + turned)) * norm)
                if i < q:
                    turned = there.T
                    spread(d, c, q * q + q + 1 + i,
                           ((back - turned) if c == 0 else (back + turned)) * norm)

    chunks = [(2, 0, groups - 1), (2, groups - 1, groups),
              (1, 0, groups - 1), (1, groups - 1, groups),
              (0, 0, groups - 2), (0, groups - 2, groups - 1), (0, groups - 1, groups)]

    def span(t):
        _, first, last = chunks[t]
        return pl.ds(first * first, last * last - first * first)

    def core_copy(t):
        d = chunks[t][0]
        return copy(keep.at[d, 1 - core, :, :, span(t)], got_core.at[d, :, :, span(t)],
                    c_send.at[t], c_recv.at[t], spot(me_w, me_x * 2 + 1 - core))

    def x_copy(t, step):
        d = chunks[t][0]
        to = lax.rem(me_x + step, across)
        return copy(part.at[d, :, to, span(t)], got_x.at[d, step - 1, :, span(t)],
                    x_send.at[t, step - 1], x_recv.at[t, step - 1], spot(me_w, to * 2 + core))

    def z_copy(t, step):
        d = chunks[t][0]
        to = lax.rem(me_z + step, outer)
        return copy(part.at[d, pl.ds(to * INNER, INNER), me_x, span(t)],
                    got_z.at[d, step - 1, :, span(t)],
                    z_send.at[t, step - 1], z_recv.at[t, step - 1], spot(to * INNER + me_y, me_n))

    def d_copy(t, step):
        d = chunks[t][0]
        to_x = lax.rem(me_x + step // wides, across)
        to_w = lax.rem(me_w + step % wides, wides)
        return copy(part.at[d, to_w, to_x, span(t)], got_d.at[step - 1],
                    d_send.at[step - 1], d_recv.at[step - 1], spot(to_w, to_x * 2 + core))

    def b_copy(t, step):
        d = chunks[t][0]
        to_y = lax.rem(me_y + step // narrows, INNER)
        to_n = lax.rem(me_n + step % narrows, narrows)
        return copy(piece.at[d, to_y, span(t)], full.at[d, me_y, me_n, span(t)],
                    b_send.at[t, step - 1], b_recv.at[t, step - 1],
                    spot(me_z * INNER + to_y, to_n))

    def core_start(t):
        core_copy(t).start()

    def core_done(t):
        d = chunks[t][0]
        core_copy(t).wait()

        def add(w, carry):
            total = keep[d, core, w, :, span(t)] + got_core[d, w, :, span(t)]
            keep[d, core, w, :, span(t)] = total
            part[d, w, :, span(t)] = total.astype(jnp.bfloat16)
            return carry

        lax.fori_loop(0, wides, add, 0)

    def x_start(t):
        core_done(t)
        for step in range(1, across):
            x_copy(t, step).start()

    def z_start(t):
        d = chunks[t][0]
        for step in range(1, across):
            x_copy(t, step).wait()

        def add(w, carry):
            total = keep[d, core, w, me_x, span(t)]
            for step in range(1, across):
                total = total + got_x[d, step - 1, w, span(t)].astype(jnp.float32)
            keep[d, core, w, me_x, span(t)] = total
            part[d, w, me_x, span(t)] = total.astype(jnp.bfloat16)
            return carry

        lax.fori_loop(0, wides, add, 0)
        for step in range(1, outer):
            z_copy(t, step).start()

    def z_done(t):
        d = chunks[t][0]
        for step in range(1, outer):
            z_copy(t, step).wait()
        for y in range(INNER):
            total = keep[d, core, me_z * INNER + y, me_x, span(t)]
            for step in range(1, outer):
                total = total + got_z[d, step - 1, y, span(t)].astype(jnp.float32)
            piece[d, y, span(t)] = total.astype(jnp.bfloat16)

    def b_start(t):
        d = chunks[t][0]
        full[d, me_y, me_n, span(t)] = piece[d, me_y, span(t)]
        for step in range(1, INNER * narrows):
            b_copy(t, step).start()

    def b_done(t):
        for step in range(1, INNER * narrows):
            b_copy(t, step).wait()

    def d_start(t):
        core_done(t)
        for step in range(1, wides * across):
            d_copy(t, step).start()

    def d_done(t):
        d = chunks[t][0]
        for step in range(1, wides * across):
            d_copy(t, step).wait()
        total = keep[d, core, me_w, me_x, span(t)]
        for step in range(1, wides * across):
            total = total + got_d[step - 1].astype(jnp.float32)
        total = total.astype(jnp.bfloat16)
        piece[d, me_y, span(t)] = total
        full[d, me_y, me_n, span(t)] = total
        for step in range(1, narrows):
            b_copy(t, step).start()

    def gather(t, direct=False):
        d, first, last = chunks[t]
        for q in range(first, last):
            for i in range(q + 1):
                pairs = [(i, q, q * q + i)] + ([(q, i, q * q + q + 1 + i)] if i < q else [])
                for at, over, b in pairs:
                    for c in range(2):
                        for x in range(across):
                            source = x * 2 + c
                            if direct:
                                value = full[d, me_y, source, b]
                            else:
                                value = full[d, 0, source, b].astype(jnp.float32)
                                for y in range(1, INNER):
                                    value = value + full[d, y, source, b].astype(jnp.float32)
                                value = value.astype(jnp.bfloat16)
                            to = at * per + x * sub
                            low[d, c, to:to + sub, over * BLOCK:(over + 1) * BLOCK] = value

    def finish(d):
        real = low[d, 0]
        imag = low[d, 1]
        elems[d, 0] = jnp.dot(real, unmix[...], preferred_element_type=jnp.float32)
        elems[d, 1] = jnp.dot(imag, unmix[...], preferred_element_type=jnp.float32)
        both = (jnp.dot(real, per_two[0], preferred_element_type=jnp.float32)
                + jnp.dot(imag, per_two[1], preferred_element_type=jnp.float32))
        prods[d, 0] = both[:, :cols]
        prods[d, 1] = both[:, cols:]

    def step(d, q):
        forward(d, q, range(planes - 1) if d == 0 else range(planes))
        if d == 0:
            halo_copies[q].wait()
            forward(d, q, range(planes - 1, planes))
        fold(d, q)

    last = groups - 1
    for q in range(last):
        step(2, q)
    core_start(0)
    step(2, last)
    core_start(1)
    row_copy.wait()
    step(1, 0)
    x_start(0)
    step(1, 1)
    x_start(1)
    for q in range(2, last):
        step(1, q)
    core_start(2)
    z_start(0)
    step(1, last)
    core_start(3)
    z_start(1)
    at_row = lax.broadcasted_iota(jnp.int32, (BLOCK, count), 0)
    at_lane = lax.broadcasted_iota(jnp.int32, (BLOCK, count), 1)
    for q in range(groups):
        target = at_row // per * rows + q * per + lax.rem(at_row, per)
        unmix[q * BLOCK:(q + 1) * BLOCK, :] = jnp.where(at_lane == target, 1.0, 0.0).astype(jnp.bfloat16)
    step(0, 0)
    x_start(2)
    for q in range(1, groups - 2):
        step(0, q)
    core_start(4)
    x_start(3)
    z_start(2)
    x_start(4)
    step(0, groups - 2)
    core_start(5)
    z_start(3)
    z_done(0)
    z_done(1)
    z_start(4)
    x_start(5)
    for one in per_copies:
        one.wait()
    step(0, last)
    core_start(6)
    b_start(0)
    b_start(1)
    for one in per_turn:
        one.start()
    d_start(6)
    z_done(2)
    z_done(3)
    b_start(2)
    b_start(3)
    z_start(5)
    z_done(4)
    b_start(4)
    for one in per_turn:
        one.wait()
    both = per_all[...].astype(jnp.float32).reshape(count, 2 * cols)
    per_two[0] = both.astype(jnp.bfloat16)
    per_two[1] = jnp.concatenate([-both[:, cols:], both[:, :cols]], 1).astype(jnp.bfloat16)
    b_done(0)
    b_done(1)
    gather(0)
    gather(1)
    finish(2)
    z_done(5)
    b_start(5)
    d_done(6)
    b_done(2)
    b_done(3)
    gather(2)
    gather(3)
    finish(1)
    b_done(4)
    gather(4)
    b_done(5)
    gather(5)
    for s in range(1, narrows):
        b_copy(6, s).wait()
    gather(6, True)
    finish(0)
    for slot in range(3):
        d = dirs[slot]
        elem_out[slot] = elems[d]
        prod_out[slot] = prods[d]


def on_device(vectors, links, directions, peram):
    count, _, _, planes, lanes = vectors.shape
    wides = lax.axis_size("wide")
    narrows = lax.axis_size("narrow")
    slots = directions.shape[0]
    cols = peram.shape[2]
    rows = count // wides
    across = narrows // 2
    groups = count // BLOCK
    per = rows // groups
    sub = per // across
    outer = wides // INNER
    blocks = groups * groups
    tail = 2 * groups - 1
    norm = 1.0 / math.sqrt(12.0 * planes * wides * lanes * narrows)
    turned = vectors.transpose(3, 1, 2, 0, 4).reshape(planes, 6, wides, rows, lanes)
    vmem = pl.BlockSpec(memory_space=pltpu.VMEM)
    low = jnp.bfloat16
    wide = jnp.float32
    dma = pltpu.SemaphoreType.DMA
    return pl.pallas_call(
        functools.partial(kernel, wides, narrows, norm),
        out_shape=(
            jax.ShapeDtypeStruct((slots, 2, rows, count), jnp.float32),
            jax.ShapeDtypeStruct((slots, 2, rows, cols), jnp.float32),
        ),
        in_specs=[vmem, vmem, pl.BlockSpec(memory_space=pltpu.SMEM), vmem],
        out_specs=(vmem, vmem),
        scratch_shapes=[
            pltpu.VMEM((planes, 6, count * LZ // lanes, lanes), low),
            pltpu.VMEM((groups, 6, wides, per, lanes), low),
            pltpu.VMEM((planes, 6, count * LZ // lanes, lanes), low),
            pltpu.VMEM((count, planes * 6 * lanes), low),
            pltpu.VMEM((2 * BLOCK, planes * 6 * lanes), low),
            pltpu.VMEM((groups, count, 2 * BLOCK), wide),
            pltpu.VMEM((3, 2, wides, across, blocks, sub, BLOCK), wide),
            pltpu.VMEM((3, wides, across, blocks, sub, BLOCK), wide),
            pltpu.VMEM((3, wides, across, blocks, sub, BLOCK), low),
            pltpu.VMEM((3, across - 1, wides, blocks, sub, BLOCK), low),
            pltpu.VMEM((3, outer - 1, INNER, blocks, sub, BLOCK), low),
            pltpu.VMEM((wides * across - 1, tail, sub, BLOCK), low),
            pltpu.VMEM((3, INNER, blocks, sub, BLOCK), low),
            pltpu.VMEM((3, INNER, narrows, blocks, sub, BLOCK), low),
            pltpu.VMEM((3, 2, rows, count), low),
            pltpu.VMEM((3, 2, rows, count), wide),
            pltpu.VMEM((3, 2, rows, cols), wide),
            pltpu.VMEM((groups, per, 2 * cols), low),
            pltpu.VMEM((groups, outer, INNER, per, 2 * cols), low),
            pltpu.VMEM((2, count, 2 * cols), low),
            pltpu.VMEM((count, count), low),
            dma((groups + 1,)), dma((groups + 1,)),
            dma((outer + INNER,)), dma((outer + INNER,)),
            dma((7,)), dma((7,)),
            dma((7, across - 1)), dma((7, across - 1)),
            dma((7, outer - 1)), dma((7, outer - 1)),
            dma((7, INNER * narrows - 1)), dma((7, INNER * narrows - 1)),
            dma((wides * across - 1,)), dma((wides * across - 1,)),
        ],
        compiler_params=pltpu.CompilerParams(
            collective_id=0, has_side_effects=True, vmem_limit_bytes=50 * 2**20),
    )(turned, links, directions, peram)


def solution(mesh):
    placed = (
        P("grp", None, None, "wide", "narrow"),
        P("grp", None, None, None, "wide", "narrow"),
        P(),
        P("grp", "wide", "narrow"),
    )
    return jax.shard_map(
        on_device,
        mesh=mesh,
        in_specs=placed,
        out_specs=(P("grp", None, "wide", None), P("grp", None, "wide", "narrow")),
        check_vma=False,
    )
```

```python
import functools
import math

import jax
import jax.numpy as jnp
from jax import lax
from jax.experimental import pallas as pl
from jax.experimental.pallas import tpu as pltpu
from jax.sharding import PartitionSpec as P

LZ = 16
ORDER = (2, 1, 0)
CHUNK = 32
INNER = 2
MESH = pl.DeviceIdType.MESH
NT = (((1,), (1,)), ((), ()))


def kernel(wides, narrows, norm, vec, links, peram, low_out, prod_out,
           pack, halo0, halo1, f_re, f_im, half, keep, part, got_core, got_row, got_wide,
           thin, full, per_own, per_all,
           h_send, h_recv, p_send, p_recv, c_send, c_recv, r_send, r_recv,
           w_send, w_recv, g_send, g_recv):
    planes, comps, count, lanes = vec.shape
    groups = lanes // LZ
    per_group = count // groups
    rows = count // wides
    share = 2 * rows // narrows
    across = narrows // 2
    me_w = lax.axis_index("wide")
    me_n = lax.axis_index("narrow")
    core = lax.rem(me_n, 2)
    me_x = me_n // 2
    outer = wides // INNER
    me_z = me_w // INNER
    me_y = lax.rem(me_w, INNER)
    cols = peram.shape[2]

    def at_wide(step):
        return {"wide": lax.rem(me_w + step, wides)}

    def at_narrow(step):
        return {"narrow": lax.rem(me_n + step, narrows)}

    def at_row(step):
        return {"narrow": lax.rem(me_x + step, across) * 2 + core}

    def copy(src, dst, send, recv, where):
        return pltpu.make_async_remote_copy(
            src_ref=src, dst_ref=dst, send_sem=send, recv_sem=recv,
            device_id=where, device_id_type=MESH)

    barrier = pltpu.get_barrier_semaphore()
    for step in range(1, wides):
        pl.semaphore_signal(barrier, inc=1, device_id=at_wide(step), device_id_type=MESH)
    for step in range(1, narrows):
        pl.semaphore_signal(barrier, inc=1, device_id=at_narrow(step), device_id_type=MESH)

    lane = lax.broadcasted_iota(jnp.int32, (CHUNK, lanes), 1)

    def pack_rows(i, carry):
        slab = i // (per_group // CHUNK)
        start = pl.multiple_of(lax.rem(i, per_group // CHUNK) * CHUNK, CHUNK)
        plane = slab // comps
        comp = lax.rem(slab, comps)
        total = jnp.zeros((CHUNK, lanes), jnp.float32)
        for group in range(groups):
            piece = vec[plane, comp, pl.ds(group * per_group + start, CHUNK), :].astype(jnp.float32)
            if group:
                piece = pltpu.roll(piece, group * LZ, 1)
            total = jnp.where(lane // LZ == group, piece, total)
        pack[plane, comp, pl.ds(start, CHUNK), :] = total.astype(jnp.bfloat16)
        return carry

    pl.semaphore_wait(barrier, wides + narrows - 2)
    first_copy = copy(vec.at[0], halo0, h_send.at[0], h_recv.at[0], at_wide(wides - 1))
    second_copy = copy(pack, halo1, h_send.at[1], h_recv.at[1], at_narrow(narrows - 1))
    first_copy.start()
    lax.fori_loop(0, planes * comps * (per_group // CHUNK), pack_rows, 0)
    second_copy.start()
    per_own[...] = jnp.concatenate([peram[c].astype(jnp.float32) for c in range(2)], 1).astype(jnp.bfloat16)
    for step in range(1, outer):
        copy(per_own, per_all.at[me_z, me_y], p_send.at[0], p_recv.at[0],
             {"wide": lax.rem(me_z + step, outer) * INNER + me_y}).start()
    per_all[me_z, me_y] = per_own[...]
    per_turn = [
        copy(per_all.at[:, me_y], per_all.at[:, me_y], p_send.at[step], p_recv.at[step],
             {"wide": me_z * INNER + lax.rem(me_y + step, INNER)})
        for step in range(1, INNER)
    ]

    def settle(ref, send, recv):
        one = copy(ref, ref, send, recv, at_wide(1))
        one.wait_send()
        one.wait_recv()

    def shifted(direction, plane, comp, start):
        here = pl.ds(start, CHUNK)
        if direction == 0:
            if plane + 1 < planes:
                return vec[plane + 1, comp, here, :].astype(jnp.float32)
            return halo0[comp, here, :].astype(jnp.float32)
        own = vec[plane, comp, here, :].astype(jnp.float32)
        if direction == 1:
            group = start // per_group
            inside = pl.multiple_of(lax.rem(start, per_group), CHUNK)
            ahead = halo1[plane, comp, pl.ds(inside, CHUNK), :].astype(jnp.float32)
            ahead = pltpu.roll(ahead, lanes - LZ - LZ * group, 1)
            return jnp.where(lane < lanes - LZ, pltpu.roll(own, lanes - LZ, 1), ahead)
        return jnp.where(
            lax.rem(lane, LZ) < LZ - 1, pltpu.roll(own, lanes - 1, 1), pltpu.roll(own, LZ - 1, 1))

    def forward(direction, planes_here=None):
        for plane in planes_here or range(planes):
            def chunk(i, carry):
                start = pl.multiple_of(i * CHUNK, CHUNK)
                values = [shifted(direction, plane, comp, start) for comp in range(comps)]
                for a in range(3):
                    real = imag = None
                    for b in range(3):
                        link_r = links[direction, 0, a, b, plane:plane + 1, :]
                        link_i = links[direction, 1, a, b, plane:plane + 1, :]
                        term_r = link_r * values[b] - link_i * values[3 + b]
                        term_i = link_r * values[3 + b] + link_i * values[b]
                        real = term_r if real is None else real + term_r
                        imag = term_i if imag is None else imag + term_i
                    real = real.astype(jnp.bfloat16)
                    imag = imag.astype(jnp.bfloat16)
                    low = (plane * comps + a) * lanes
                    high = low + 3 * lanes
                    f_re[pl.ds(start, CHUNK), low:low + lanes] = real
                    f_re[pl.ds(start, CHUNK), high:high + lanes] = imag
                    f_im[pl.ds(start, CHUNK), low:low + lanes] = imag
                    f_im[pl.ds(start, CHUNK), high:high + lanes] = -real
                return carry

            lax.fori_loop(0, count // CHUNK, chunk, 0)

    def compute(direction):
        left = jnp.concatenate(
            [vec[plane, comp] for plane in range(planes) for comp in range(comps)], 1)
        half[0] = lax.dot_general(left, f_re[...], NT, preferred_element_type=jnp.float32)
        half[1] = lax.dot_general(left, f_im[...], NT, preferred_element_type=jnp.float32)
        block = lanes
        for c in range(2):
            for top in range(0, count, block):
                turned = half[c, :, top:top + block].T
                own = half[c, top:top + block, :]
                terms = ((own - turned) if c == 0 else (own + turned)) * norm
                for low in range(0, block, share):
                    row = top + low
                    owner = c * across + (row % rows) // share
                    piece = terms[low:low + share]
                    keep[direction, owner % 2, owner // 2, row // rows] = piece
                    part[direction, owner % 2, owner // 2, row // rows] = piece.astype(jnp.bfloat16)

    def core_copy(d):
        return copy(part.at[d, 1 - core], got_core.at[d], c_send.at[d], c_recv.at[d],
                    {"narrow": me_x * 2 + 1 - core})

    def row_copy(d, step):
        return copy(part.at[d, core, lax.rem(me_x + step, across)], got_row.at[d, step - 1],
                    r_send.at[d], r_recv.at[d], at_row(step))

    def wide_copy(d, step):
        return copy(part.at[d, core, me_x, lax.rem(me_w + step, wides)],
                    got_wide.at[d, step - 1],
                    w_send.at[d], w_recv.at[d], at_wide(step))

    def full_copy(d, step):
        return copy(thin.at[d], full.at[d, me_n], g_send.at[d], g_recv.at[d],
                    at_narrow(step))

    def core_done(d):
        core_copy(d).wait()
        for x in range(across):
            def add(w, carry):
                total = keep[d, core, x, w] + got_core[d, x, w].astype(jnp.float32)
                keep[d, core, x, w] = total
                part[d, core, x, w] = total.astype(jnp.bfloat16)
                return carry
            lax.fori_loop(0, wides, add, 0)
        for step in range(1, across):
            row_copy(d, step).start()

    def row_done(d):
        settle(got_row.at[d], r_send.at[d], r_recv.at[d])

        def add(w, carry):
            total = keep[d, core, me_x, w]
            for step in range(1, across):
                total = total + got_row[d, step - 1, w].astype(jnp.float32)
            keep[d, core, me_x, w] = total
            part[d, core, me_x, w] = total.astype(jnp.bfloat16)
            return carry

        lax.fori_loop(0, wides, add, 0)
        for step in range(1, wides):
            wide_copy(d, step).start()

    def wide_done(d):
        settle(got_wide.at[d], w_send.at[d], w_recv.at[d])
        total = keep[d, core, me_x, me_w]
        for step in range(1, wides):
            total = total + got_wide[d, step - 1].astype(jnp.float32)
        total = total.astype(jnp.bfloat16)
        thin[d] = total
        full[d, me_n] = total
        for step in range(1, narrows):
            full_copy(d, step).start()

    def finish(d):
        settle(full.at[d, 0:narrows - 1], g_send.at[d], g_recv.at[d])
        real = full[d, 0:across].astype(jnp.float32).reshape(rows, count).astype(jnp.bfloat16)
        imag = full[d, across:narrows].astype(jnp.float32).reshape(rows, count).astype(jnp.bfloat16)
        low_out[d, 0] = real
        low_out[d, 1] = imag
        both = per_all[...].astype(jnp.float32).reshape(count, 2 * cols).astype(jnp.bfloat16)

        def times(x):
            return jnp.dot(x, both, preferred_element_type=jnp.float32)

        first = times(real)
        second = times(imag)
        prod_out[d, 0] = first[:, :cols] - second[:, cols:]
        prod_out[d, 1] = first[:, cols:] + second[:, :cols]

    forward(2)
    compute(2)
    core_copy(2).start()
    second_copy.wait()
    forward(1)
    core_done(2)
    compute(1)
    core_copy(1).start()
    forward(0, range(planes - 1))
    core_done(1)
    row_done(2)
    first_copy.wait()
    settle(per_all.at[0:outer - 1, 0], p_send.at[0], p_recv.at[0])
    for one in per_turn:
        one.start()
    forward(0, range(planes - 1, planes))
    compute(0)
    core_copy(0).start()
    core_done(0)
    row_done(1)
    wide_done(2)
    row_done(0)
    for one in per_turn:
        one.wait()
    wide_done(1)
    finish(2)
    wide_done(0)
    finish(1)
    finish(0)


def place(dirs, low, prods, elem_out, prod_out, elems, held, sems):
    slots = elems.shape[0]
    copies = []
    for slot in range(slots):
        chosen = dirs[0:1, slot:slot + 1]
        value = low[0].astype(jnp.float32)
        other = prods[0]
        for d in range(1, slots):
            value = jnp.where(chosen[None] == d, low[d].astype(jnp.float32), value)
            other = jnp.where(chosen[None] == d, prods[d], other)
        elems[slot] = value
        copies.append(pltpu.make_async_copy(elems.at[slot], elem_out.at[slot], sems.at[slot]))
        copies[-1].start()
        held[slot] = other
    copies.append(pltpu.make_async_copy(held, prod_out, sems.at[slots]))
    copies[-1].start()
    for one in copies:
        one.wait()


def on_device(vectors, links, directions, peram):
    count, _, _, planes, lanes = vectors.shape
    wides = lax.axis_size("wide")
    narrows = lax.axis_size("narrow")
    slots = directions.shape[0]
    cols = peram.shape[2]
    rows = count // wides
    share = 2 * rows // narrows
    across = narrows // 2
    norm = 1.0 / math.sqrt(12.0 * planes * wides * lanes * narrows)
    turned = vectors.transpose(3, 1, 2, 0, 4).reshape(planes, 6, count, lanes)
    vmem = pl.BlockSpec(memory_space=pltpu.VMEM)
    low = jnp.bfloat16
    dma = pltpu.SemaphoreType.DMA
    lows, prods = pl.pallas_call(
        functools.partial(kernel, wides, narrows, norm),
        out_shape=(
            jax.ShapeDtypeStruct((slots, 2, rows, count), jnp.bfloat16),
            jax.ShapeDtypeStruct((slots, 2, rows, cols), jnp.float32),
        ),
        in_specs=[vmem, vmem, vmem],
        out_specs=(vmem, vmem),
        scratch_shapes=[
            pltpu.VMEM((planes, 6, count * LZ // lanes, lanes), low),
            pltpu.VMEM((6, count, lanes), low),
            pltpu.VMEM((planes, 6, count * LZ // lanes, lanes), low),
            pltpu.VMEM((count, planes * 6 * lanes), low),
            pltpu.VMEM((count, planes * 6 * lanes), low),
            pltpu.VMEM((2, count, count), jnp.float32),
            pltpu.VMEM((3, 2, across, wides, share, count), jnp.float32),
            pltpu.VMEM((3, 2, across, wides, share, count), low),
            pltpu.VMEM((3, across, wides, share, count), low),
            pltpu.VMEM((3, across - 1, wides, share, count), low),
            pltpu.VMEM((3, wides - 1, share, count), low),
            pltpu.VMEM((3, share, count), low),
            pltpu.VMEM((3, narrows, share, count), low),
            pltpu.VMEM((rows, 2 * cols), low),
            pltpu.VMEM((wides // INNER, INNER, rows, 2 * cols), low),
            dma((2,)), dma((2,)),
            dma((INNER,)), dma((INNER,)),
            dma((3,)), dma((3,)),
            dma((3,)), dma((3,)),
            dma((3,)), dma((3,)),
            dma((3,)), dma((3,)),
        ],
        compiler_params=pltpu.CompilerParams(
            collective_id=0, has_side_effects=True, vmem_limit_bytes=50 * 2**20),
    )(turned, links, peram)
    anywhere = pl.BlockSpec(memory_space=pl.ANY)
    return pl.pallas_call(
        place,
        out_shape=(
            jax.ShapeDtypeStruct((slots, 2, rows, count), jnp.float32),
            jax.ShapeDtypeStruct((slots, 2, rows, cols), jnp.float32),
        ),
        in_specs=[vmem, vmem, vmem],
        out_specs=(anywhere, anywhere),
        scratch_shapes=[
            pltpu.VMEM((slots, 2, rows, count), jnp.float32),
            pltpu.VMEM((slots, 2, rows, cols), jnp.float32),
            dma((slots + 1,)),
        ],
        compiler_params=pltpu.CompilerParams(vmem_limit_bytes=8 * 2**20),
    )(directions.reshape(1, slots), lows, prods)


def solution(mesh):
    placed = (
        P("grp", None, None, "wide", "narrow"),
        P("grp", None, None, None, "wide", "narrow"),
        P(),
        P("grp", "wide", "narrow"),
    )
    return jax.shard_map(
        on_device,
        mesh=mesh,
        in_specs=placed,
        out_specs=(P("grp", None, "wide", None), P("grp", None, "wide", "narrow")),
        check_vma=False,
    )
```

```python
import functools
import math

import jax
import jax.numpy as jnp
from jax import lax
from jax.experimental import pallas as pl
from jax.experimental.pallas import tpu as pltpu
from jax.sharding import PartitionSpec as P

LZ = 16
ORDER = (2, 1, 0)
CHUNK = 32
BLOCK = 128
INNER = 2
MESH = pl.DeviceIdType.MESH
NT = (((1,), (1,)), ((), ()))


def kernel(wides, narrows, norm, vec, links, peram, low_out, prod_out,
           pack, halo0, halo1, f_re, f_im, half, keep, part, got_core, got_row, got_wide,
           thin, full, per_own, per_all,
           h_send, h_recv, p_send, p_recv, c_send, c_recv, r_send, r_recv,
           w_send, w_recv, g_send, g_recv):
    planes, comps, count, lanes = vec.shape
    groups = lanes // LZ
    per_group = count // groups
    rows = count // wides
    share = 2 * rows // narrows
    across = narrows // 2
    me_w = lax.axis_index("wide")
    me_n = lax.axis_index("narrow")
    core = lax.rem(me_n, 2)
    me_x = me_n // 2
    outer = wides // INNER
    me_z = me_w // INNER
    me_y = lax.rem(me_w, INNER)
    cols = peram.shape[2]

    def at_wide(step):
        return {"wide": lax.rem(me_w + step, wides)}

    def at_narrow(step):
        return {"narrow": lax.rem(me_n + step, narrows)}

    def at_row(step):
        return {"narrow": lax.rem(me_x + step, across) * 2 + core}

    def copy(src, dst, send, recv, where):
        return pltpu.make_async_remote_copy(
            src_ref=src, dst_ref=dst, send_sem=send, recv_sem=recv,
            device_id=where, device_id_type=MESH)

    barrier = pltpu.get_barrier_semaphore()
    for step in range(1, wides):
        pl.semaphore_signal(barrier, inc=1, device_id=at_wide(step), device_id_type=MESH)
    for step in range(1, narrows):
        pl.semaphore_signal(barrier, inc=1, device_id=at_narrow(step), device_id_type=MESH)

    lane = lax.broadcasted_iota(jnp.int32, (CHUNK, lanes), 1)

    def pack_rows(i, carry):
        slab = i // (per_group // CHUNK)
        start = pl.multiple_of(lax.rem(i, per_group // CHUNK) * CHUNK, CHUNK)
        plane = slab // comps
        comp = lax.rem(slab, comps)
        total = jnp.zeros((CHUNK, lanes), jnp.float32)
        for group in range(groups):
            piece = vec[plane, comp, pl.ds(group * per_group + start, CHUNK), :].astype(jnp.float32)
            if group:
                piece = pltpu.roll(piece, group * LZ, 1)
            total = jnp.where(lane // LZ == group, piece, total)
        pack[plane, comp, pl.ds(start, CHUNK), :] = total.astype(jnp.bfloat16)
        return carry

    pl.semaphore_wait(barrier, wides + narrows - 2)
    blocks = count // BLOCK

    def first_copy(q):
        here = pl.ds(q * BLOCK if isinstance(q, int) else pl.multiple_of(q * BLOCK, BLOCK), BLOCK)
        return copy(vec.at[0, :, here, :], halo0.at[:, here, :], h_send.at[q], h_recv.at[q],
                    at_wide(wides - 1))

    second_copy = copy(pack, halo1, h_send.at[blocks], h_recv.at[blocks], at_narrow(narrows - 1))
    for q in range(blocks):
        first_copy(q).start()
    lax.fori_loop(0, planes * comps * (per_group // CHUNK), pack_rows, 0)
    second_copy.start()
    per_own[...] = jnp.concatenate([peram[c].astype(jnp.float32) for c in range(2)], 1).astype(jnp.bfloat16)
    for step in range(1, outer):
        copy(per_own, per_all.at[me_z, me_y], p_send.at[0], p_recv.at[0],
             {"wide": lax.rem(me_z + step, outer) * INNER + me_y}).start()
    per_all[me_z, me_y] = per_own[...]
    per_turn = [
        copy(per_all.at[:, me_y], per_all.at[:, me_y], p_send.at[step], p_recv.at[step],
             {"wide": me_z * INNER + lax.rem(me_y + step, INNER)})
        for step in range(1, INNER)
    ]

    def settle(ref, send, recv):
        one = copy(ref, ref, send, recv, at_wide(1))
        one.wait_send()
        one.wait_recv()

    def shifted(direction, plane, comp, start):
        here = pl.ds(start, CHUNK)
        if direction == 0:
            if plane + 1 < planes:
                return vec[plane + 1, comp, here, :].astype(jnp.float32)
            return halo0[comp, here, :].astype(jnp.float32)
        own = vec[plane, comp, here, :].astype(jnp.float32)
        if direction == 1:
            group = start // per_group
            inside = pl.multiple_of(lax.rem(start, per_group), CHUNK)
            ahead = halo1[plane, comp, pl.ds(inside, CHUNK), :].astype(jnp.float32)
            ahead = pltpu.roll(ahead, lanes - LZ - LZ * group, 1)
            return jnp.where(lane < lanes - LZ, pltpu.roll(own, lanes - LZ, 1), ahead)
        return jnp.where(
            lax.rem(lane, LZ) < LZ - 1, pltpu.roll(own, lanes - 1, 1), pltpu.roll(own, LZ - 1, 1))

    def forward(direction, planes_here=None, first=0, past=count):
        for plane in planes_here or range(planes):
            def chunk(i, carry):
                start = pl.multiple_of(i * CHUNK, CHUNK)
                values = [shifted(direction, plane, comp, start) for comp in range(comps)]
                for a in range(3):
                    real = imag = None
                    for b in range(3):
                        link_r = links[direction, 0, a, b, plane:plane + 1, :]
                        link_i = links[direction, 1, a, b, plane:plane + 1, :]
                        term_r = link_r * values[b] - link_i * values[3 + b]
                        term_i = link_r * values[3 + b] + link_i * values[b]
                        real = term_r if real is None else real + term_r
                        imag = term_i if imag is None else imag + term_i
                    real = real.astype(jnp.bfloat16)
                    imag = imag.astype(jnp.bfloat16)
                    low = (plane * comps + a) * lanes
                    high = low + 3 * lanes
                    f_re[pl.ds(start, CHUNK), low:low + lanes] = real
                    f_re[pl.ds(start, CHUNK), high:high + lanes] = imag
                    f_im[pl.ds(start, CHUNK), low:low + lanes] = imag
                    f_im[pl.ds(start, CHUNK), high:high + lanes] = -real
                return carry

            lax.fori_loop(first // CHUNK, past // CHUNK, chunk, 0)

    inside = (planes - 1) * comps * lanes

    def columns(planes_here):
        return jnp.concatenate([vec[plane, comp] for plane in planes_here for comp in range(comps)], 1)

    def compute(direction):
        left = columns(range(planes))
        half[0] = lax.dot_general(left, f_re[...], NT, preferred_element_type=jnp.float32)
        half[1] = lax.dot_general(left, f_im[...], NT, preferred_element_type=jnp.float32)

    def compute_inside():
        left = columns(range(planes - 1))
        half[0] = lax.dot_general(left, f_re[:, :inside], NT, preferred_element_type=jnp.float32)
        half[1] = lax.dot_general(left, f_im[:, :inside], NT, preferred_element_type=jnp.float32)

    def compute_block(q, carry):
        first_copy(q).wait()
        here = pl.ds(pl.multiple_of(q * BLOCK, BLOCK), BLOCK)
        forward(0, range(planes - 1, planes), q * BLOCK, q * BLOCK + BLOCK)
        right = jnp.concatenate([f_re[here, inside:], f_im[here, inside:]], 0)
        both = lax.dot_general(
            columns(range(planes - 1, planes)), right, NT, preferred_element_type=jnp.float32)
        for c in range(2):
            half[c, :, here] = half[c, :, here] + both[:, c * BLOCK:(c + 1) * BLOCK]
        return carry

    def fold(direction):
        block = lanes
        for c in range(2):
            for top in range(0, count, block):
                turned = half[c, :, top:top + block].T
                own = half[c, top:top + block, :]
                terms = ((own - turned) if c == 0 else (own + turned)) * norm
                for low in range(0, block, share):
                    row = top + low
                    owner = c * across + (row % rows) // share
                    piece = terms[low:low + share]
                    keep[direction, owner % 2, owner // 2, row // rows] = piece
                    part[direction, owner % 2, owner // 2, row // rows] = piece.astype(jnp.bfloat16)
            core_copy(direction, c).start()

    def core_copy(d, c):
        here = pl.ds(c * (across // 2), across // 2)
        return copy(part.at[d, 1 - core, here], got_core.at[d, here], c_send.at[d, c], c_recv.at[d, c],
                    {"narrow": me_x * 2 + 1 - core})

    def row_copy(d, step):
        return copy(part.at[d, core, lax.rem(me_x + step, across)], got_row.at[d, step - 1],
                    r_send.at[d], r_recv.at[d], at_row(step))

    def wide_copy(d, step):
        return copy(part.at[d, core, me_x, lax.rem(me_w + step, wides)],
                    got_wide.at[d, step - 1],
                    w_send.at[d], w_recv.at[d], at_wide(step))

    def full_copy(d, step):
        return copy(thin.at[d], full.at[d, me_n], g_send.at[d], g_recv.at[d],
                    at_narrow(step))

    def core_done(d):
        for c in range(2):
            core_copy(d, c).wait()
        for x in range(across):
            def add(w, carry):
                total = keep[d, core, x, w] + got_core[d, x, w].astype(jnp.float32)
                keep[d, core, x, w] = total
                part[d, core, x, w] = total.astype(jnp.bfloat16)
                return carry
            lax.fori_loop(0, wides, add, 0)
        for step in range(1, across):
            row_copy(d, step).start()

    def row_done(d):
        settle(got_row.at[d], r_send.at[d], r_recv.at[d])

        def add(w, carry):
            total = keep[d, core, me_x, w]
            for step in range(1, across):
                total = total + got_row[d, step - 1, w].astype(jnp.float32)
            keep[d, core, me_x, w] = total
            part[d, core, me_x, w] = total.astype(jnp.bfloat16)
            return carry

        lax.fori_loop(0, wides, add, 0)
        for step in range(1, wides):
            wide_copy(d, step).start()

    def wide_done(d):
        settle(got_wide.at[d], w_send.at[d], w_recv.at[d])
        total = keep[d, core, me_x, me_w]
        for step in range(1, wides):
            total = total + got_wide[d, step - 1].astype(jnp.float32)
        total = total.astype(jnp.bfloat16)
        thin[d] = total
        full[d, me_n] = total
        for step in range(1, narrows):
            full_copy(d, step).start()

    def finish(d):
        settle(full.at[d, 0:narrows - 1], g_send.at[d], g_recv.at[d])
        real = full[d, 0:across].astype(jnp.float32).reshape(rows, count).astype(jnp.bfloat16)
        imag = full[d, across:narrows].astype(jnp.float32).reshape(rows, count).astype(jnp.bfloat16)
        low_out[d, 0] = real
        low_out[d, 1] = imag
        both = per_all[...].astype(jnp.float32).reshape(count, 2 * cols).astype(jnp.bfloat16)

        def times(x):
            return jnp.dot(x, both, preferred_element_type=jnp.float32)

        first = times(real)
        second = times(imag)
        prod_out[d, 0] = first[:, :cols] - second[:, cols:]
        prod_out[d, 1] = first[:, cols:] + second[:, :cols]

    forward(2)
    compute(2)
    fold(2)
    second_copy.wait()
    forward(1)
    core_done(2)
    compute(1)
    fold(1)
    forward(0, range(planes - 1))
    compute_inside()
    core_done(1)
    lax.fori_loop(0, blocks, compute_block, 0)
    fold(0)
    row_done(2)
    settle(per_all.at[0:outer - 1, 0], p_send.at[0], p_recv.at[0])
    for one in per_turn:
        one.start()
    core_done(0)
    row_done(1)
    wide_done(2)
    row_done(0)
    for one in per_turn:
        one.wait()
    wide_done(1)
    finish(2)
    wide_done(0)
    finish(1)
    finish(0)


def place(dirs, low, prods, elem_out, prod_out, elems, held, sems):
    slots = elems.shape[0]
    copies = []
    for slot in range(slots):
        chosen = dirs[0:1, slot:slot + 1]
        value = low[0].astype(jnp.float32)
        other = prods[0]
        for d in range(1, slots):
            value = jnp.where(chosen[None] == d, low[d].astype(jnp.float32), value)
            other = jnp.where(chosen[None] == d, prods[d], other)
        elems[slot] = value
        copies.append(pltpu.make_async_copy(elems.at[slot], elem_out.at[slot], sems.at[slot]))
        copies[-1].start()
        held[slot] = other
    copies.append(pltpu.make_async_copy(held, prod_out, sems.at[slots]))
    copies[-1].start()
    for one in copies:
        one.wait()


def on_device(vectors, links, directions, peram):
    count, _, _, planes, lanes = vectors.shape
    wides = lax.axis_size("wide")
    narrows = lax.axis_size("narrow")
    slots = directions.shape[0]
    cols = peram.shape[2]
    rows = count // wides
    share = 2 * rows // narrows
    across = narrows // 2
    norm = 1.0 / math.sqrt(12.0 * planes * wides * lanes * narrows)
    turned = vectors.transpose(3, 1, 2, 0, 4).reshape(planes, 6, count, lanes)
    vmem = pl.BlockSpec(memory_space=pltpu.VMEM)
    low = jnp.bfloat16
    dma = pltpu.SemaphoreType.DMA
    lows, prods = pl.pallas_call(
        functools.partial(kernel, wides, narrows, norm),
        out_shape=(
            jax.ShapeDtypeStruct((slots, 2, rows, count), jnp.bfloat16),
            jax.ShapeDtypeStruct((slots, 2, rows, cols), jnp.float32),
        ),
        in_specs=[vmem, vmem, vmem],
        out_specs=(vmem, vmem),
        scratch_shapes=[
            pltpu.VMEM((planes, 6, count * LZ // lanes, lanes), low),
            pltpu.VMEM((6, count, lanes), low),
            pltpu.VMEM((planes, 6, count * LZ // lanes, lanes), low),
            pltpu.VMEM((count, planes * 6 * lanes), low),
            pltpu.VMEM((count, planes * 6 * lanes), low),
            pltpu.VMEM((2, count, count), jnp.float32),
            pltpu.VMEM((3, 2, across, wides, share, count), jnp.float32),
            pltpu.VMEM((3, 2, across, wides, share, count), low),
            pltpu.VMEM((3, across, wides, share, count), low),
            pltpu.VMEM((3, across - 1, wides, share, count), low),
            pltpu.VMEM((3, wides - 1, share, count), low),
            pltpu.VMEM((3, share, count), low),
            pltpu.VMEM((3, narrows, share, count), low),
            pltpu.VMEM((rows, 2 * cols), low),
            pltpu.VMEM((wides // INNER, INNER, rows, 2 * cols), low),
            dma((count // BLOCK + 1,)), dma((count // BLOCK + 1,)),
            dma((INNER,)), dma((INNER,)),
            dma((3, 2)), dma((3, 2)),
            dma((3,)), dma((3,)),
            dma((3,)), dma((3,)),
            dma((3,)), dma((3,)),
        ],
        compiler_params=pltpu.CompilerParams(
            collective_id=0, has_side_effects=True, vmem_limit_bytes=50 * 2**20),
    )(turned, links, peram)
    anywhere = pl.BlockSpec(memory_space=pl.ANY)
    return pl.pallas_call(
        place,
        out_shape=(
            jax.ShapeDtypeStruct((slots, 2, rows, count), jnp.float32),
            jax.ShapeDtypeStruct((slots, 2, rows, cols), jnp.float32),
        ),
        in_specs=[vmem, vmem, vmem],
        out_specs=(anywhere, anywhere),
        scratch_shapes=[
            pltpu.VMEM((slots, 2, rows, count), jnp.float32),
            pltpu.VMEM((slots, 2, rows, cols), jnp.float32),
            dma((slots + 1,)),
        ],
        compiler_params=pltpu.CompilerParams(vmem_limit_bytes=8 * 2**20),
    )(directions.reshape(1, slots), lows, prods)


def solution(mesh):
    placed = (
        P("grp", None, None, "wide", "narrow"),
        P("grp", None, None, None, "wide", "narrow"),
        P(),
        P("grp", "wide", "narrow"),
    )
    return jax.shard_map(
        on_device,
        mesh=mesh,
        in_specs=placed,
        out_specs=(P("grp", None, "wide", None), P("grp", None, "wide", "narrow")),
        check_vma=False,
    )
```

```python
import functools
import math

import jax
import jax.numpy as jnp
from jax import lax
from jax.experimental import pallas as pl
from jax.experimental.pallas import tpu as pltpu
from jax.sharding import PartitionSpec as P

LZ = 16
ORDER = (2, 1, 0)
CHUNK = 32
BLOCK = 128
INNER = 2
MESH = pl.DeviceIdType.MESH
NT = (((1,), (1,)), ((), ()))


def kernel(wides, narrows, norm, vec, links, peram, low_out, prod_out,
           pack, halo0, halo1, f_re, f_im, half, keep, part, got_core, got_row, got_wide,
           thin, full, per_own, per_all,
           h_send, h_recv, p_send, p_recv, c_send, c_recv, r_send, r_recv,
           w_send, w_recv, g_send, g_recv):
    planes, comps, count, lanes = vec.shape
    groups = lanes // LZ
    per_group = count // groups
    rows = count // wides
    share = 2 * rows // narrows
    across = narrows // 2
    me_w = lax.axis_index("wide")
    me_n = lax.axis_index("narrow")
    core = lax.rem(me_n, 2)
    me_x = me_n // 2
    outer = wides // INNER
    me_z = me_w // INNER
    me_y = lax.rem(me_w, INNER)
    cols = peram.shape[2]

    def at_wide(step):
        return {"wide": lax.rem(me_w + step, wides)}

    def at_narrow(step):
        return {"narrow": lax.rem(me_n + step, narrows)}

    def at_row(step):
        return {"narrow": lax.rem(me_x + step, across) * 2 + core}

    def copy(src, dst, send, recv, where):
        return pltpu.make_async_remote_copy(
            src_ref=src, dst_ref=dst, send_sem=send, recv_sem=recv,
            device_id=where, device_id_type=MESH)

    barrier = pltpu.get_barrier_semaphore()
    for step in range(1, wides):
        pl.semaphore_signal(barrier, inc=1, device_id=at_wide(step), device_id_type=MESH)
    for step in range(1, narrows):
        pl.semaphore_signal(barrier, inc=1, device_id=at_narrow(step), device_id_type=MESH)

    lane = lax.broadcasted_iota(jnp.int32, (CHUNK, lanes), 1)

    def pack_rows(i, carry):
        slab = i // (per_group // CHUNK)
        start = pl.multiple_of(lax.rem(i, per_group // CHUNK) * CHUNK, CHUNK)
        plane = slab // comps
        comp = lax.rem(slab, comps)
        total = jnp.zeros((CHUNK, lanes), jnp.float32)
        for group in range(groups):
            piece = vec[plane, comp, pl.ds(group * per_group + start, CHUNK), :].astype(jnp.float32)
            if group:
                piece = pltpu.roll(piece, group * LZ, 1)
            total = jnp.where(lane // LZ == group, piece, total)
        pack[plane, comp, pl.ds(start, CHUNK), :] = total.astype(jnp.bfloat16)
        return carry

    pl.semaphore_wait(barrier, wides + narrows - 2)
    blocks = count // BLOCK

    def first_copy(q):
        here = pl.ds(q * BLOCK if isinstance(q, int) else pl.multiple_of(q * BLOCK, BLOCK), BLOCK)
        return copy(vec.at[0, :, here, :], halo0.at[:, here, :], h_send.at[q], h_recv.at[q],
                    at_wide(wides - 1))

    second_copy = copy(pack, halo1, h_send.at[blocks], h_recv.at[blocks], at_narrow(narrows - 1))
    for q in range(blocks):
        first_copy(q).start()
    lax.fori_loop(0, planes * comps * (per_group // CHUNK), pack_rows, 0)
    second_copy.start()
    per_own[...] = jnp.concatenate([peram[c].astype(jnp.float32) for c in range(2)], 1).astype(jnp.bfloat16)
    for step in range(1, outer):
        copy(per_own, per_all.at[me_z, me_y], p_send.at[0], p_recv.at[0],
             {"wide": lax.rem(me_z + step, outer) * INNER + me_y}).start()
    per_all[me_z, me_y] = per_own[...]
    per_turn = [
        copy(per_all.at[:, me_y], per_all.at[:, me_y], p_send.at[step], p_recv.at[step],
             {"wide": me_z * INNER + lax.rem(me_y + step, INNER)})
        for step in range(1, INNER)
    ]

    def settle(ref, send, recv):
        one = copy(ref, ref, send, recv, at_wide(1))
        one.wait_send()
        one.wait_recv()

    def shifted(direction, plane, comp, start):
        here = pl.ds(start, CHUNK)
        if direction == 0:
            if plane + 1 < planes:
                return vec[plane + 1, comp, here, :].astype(jnp.float32)
            return halo0[comp, here, :].astype(jnp.float32)
        own = vec[plane, comp, here, :].astype(jnp.float32)
        if direction == 1:
            group = start // per_group
            inside = pl.multiple_of(lax.rem(start, per_group), CHUNK)
            ahead = halo1[plane, comp, pl.ds(inside, CHUNK), :].astype(jnp.float32)
            ahead = pltpu.roll(ahead, lanes - LZ - LZ * group, 1)
            return jnp.where(lane < lanes - LZ, pltpu.roll(own, lanes - LZ, 1), ahead)
        return jnp.where(
            lax.rem(lane, LZ) < LZ - 1, pltpu.roll(own, lanes - 1, 1), pltpu.roll(own, LZ - 1, 1))

    def forward(direction, planes_here=None, first=0, past=count):
        for plane in planes_here or range(planes):
            def chunk(i, carry):
                start = pl.multiple_of(i * CHUNK, CHUNK)
                values = [shifted(direction, plane, comp, start) for comp in range(comps)]
                for a in range(3):
                    real = imag = None
                    for b in range(3):
                        link_r = links[direction, 0, a, b, plane:plane + 1, :]
                        link_i = links[direction, 1, a, b, plane:plane + 1, :]
                        term_r = link_r * values[b] - link_i * values[3 + b]
                        term_i = link_r * values[3 + b] + link_i * values[b]
                        real = term_r if real is None else real + term_r
                        imag = term_i if imag is None else imag + term_i
                    real = real.astype(jnp.bfloat16)
                    imag = imag.astype(jnp.bfloat16)
                    low = (plane * comps + a) * lanes
                    high = low + 3 * lanes
                    f_re[pl.ds(start, CHUNK), low:low + lanes] = real
                    f_re[pl.ds(start, CHUNK), high:high + lanes] = imag
                    f_im[pl.ds(start, CHUNK), low:low + lanes] = imag
                    f_im[pl.ds(start, CHUNK), high:high + lanes] = -real
                return carry

            lax.fori_loop(first // CHUNK, past // CHUNK, chunk, 0)

    inside = (planes - 1) * comps * lanes

    def columns(planes_here):
        return jnp.concatenate([vec[plane, comp] for plane in planes_here for comp in range(comps)], 1)

    def compute(direction):
        left = columns(range(planes))
        half[0] = lax.dot_general(left, f_re[...], NT, preferred_element_type=jnp.float32)
        half[1] = lax.dot_general(left, f_im[...], NT, preferred_element_type=jnp.float32)

    def compute_inside():
        left = columns(range(planes - 1))
        half[0] = lax.dot_general(left, f_re[:, :inside], NT, preferred_element_type=jnp.float32)
        half[1] = lax.dot_general(left, f_im[:, :inside], NT, preferred_element_type=jnp.float32)

    def compute_block(q, carry):
        first_copy(q).wait()
        here = pl.ds(pl.multiple_of(q * BLOCK, BLOCK), BLOCK)
        forward(0, range(planes - 1, planes), q * BLOCK, q * BLOCK + BLOCK)
        right = jnp.concatenate([f_re[here, inside:], f_im[here, inside:]], 0)
        both = lax.dot_general(
            columns(range(planes - 1, planes)), right, NT, preferred_element_type=jnp.float32)
        for c in range(2):
            half[c, :, here] = half[c, :, here] + both[:, c * BLOCK:(c + 1) * BLOCK]
        return carry

    def fold(direction):
        block = lanes
        for c in range(2):
            for top in range(0, count, block):
                turned = half[c, :, top:top + block].T
                own = half[c, top:top + block, :]
                terms = ((own - turned) if c == 0 else (own + turned)) * norm
                for low in range(0, block, share):
                    row = top + low
                    owner = c * across + (row % rows) // share
                    piece = terms[low:low + share]
                    keep[direction, owner % 2, owner // 2, row // rows] = piece
                    part[direction, owner % 2, owner // 2, row // rows] = piece.astype(jnp.bfloat16)
            core_copy(direction, c).start()

    def core_copy(d, c):
        here = pl.ds(c * (across // 2), across // 2)
        return copy(part.at[d, 1 - core, here], got_core.at[d, here], c_send.at[d, c], c_recv.at[d, c],
                    {"narrow": me_x * 2 + 1 - core})

    def row_copy(d, step):
        return copy(part.at[d, core, lax.rem(me_x + step, across)], got_row.at[d, step - 1],
                    r_send.at[d], r_recv.at[d], at_row(step))

    def wide_copy(d, step):
        return copy(part.at[d, core, me_x, lax.rem(me_w + step, wides)],
                    got_wide.at[d, step - 1],
                    w_send.at[d], w_recv.at[d], at_wide(step))

    def full_copy(d, step):
        return copy(thin.at[d], full.at[d, me_n], g_send.at[d], g_recv.at[d],
                    at_narrow(step))

    def core_done(d):
        for c in range(2):
            core_copy(d, c).wait()
        for x in range(across):
            def add(w, carry):
                total = keep[d, core, x, w] + got_core[d, x, w].astype(jnp.float32)
                keep[d, core, x, w] = total
                part[d, core, x, w] = total.astype(jnp.bfloat16)
                return carry
            lax.fori_loop(0, wides, add, 0)
        for step in range(1, across):
            row_copy(d, step).start()

    def row_done(d):
        settle(got_row.at[d], r_send.at[d], r_recv.at[d])

        def add(w, carry):
            total = keep[d, core, me_x, w]
            for step in range(1, across):
                total = total + got_row[d, step - 1, w].astype(jnp.float32)
            keep[d, core, me_x, w] = total
            part[d, core, me_x, w] = total.astype(jnp.bfloat16)
            return carry

        lax.fori_loop(0, wides, add, 0)
        for step in range(1, wides):
            wide_copy(d, step).start()

    def wide_done(d):
        settle(got_wide.at[d], w_send.at[d], w_recv.at[d])
        total = keep[d, core, me_x, me_w]
        for step in range(1, wides):
            total = total + got_wide[d, step - 1].astype(jnp.float32)
        total = total.astype(jnp.bfloat16)
        thin[d] = total
        full[d, me_n] = total
        for step in range(1, narrows):
            full_copy(d, step).start()

    def finish(d):
        settle(full.at[d, 0:narrows - 1], g_send.at[d], g_recv.at[d])
        real = full[d, 0:across].astype(jnp.float32).reshape(rows, count).astype(jnp.bfloat16)
        imag = full[d, across:narrows].astype(jnp.float32).reshape(rows, count).astype(jnp.bfloat16)
        low_out[d, 0] = real
        low_out[d, 1] = imag
        both = per_all[...].astype(jnp.float32).reshape(count, 2 * cols).astype(jnp.bfloat16)

        def times(x):
            return jnp.dot(x, both, preferred_element_type=jnp.float32)

        first = times(real)
        second = times(imag)
        prod_out[d, 0] = first[:, :cols] - second[:, cols:]
        prod_out[d, 1] = first[:, cols:] + second[:, :cols]

    forward(2)
    compute(2)
    fold(2)
    second_copy.wait()
    forward(1)
    core_done(2)
    compute(1)
    fold(1)
    forward(0, range(planes - 1))
    compute_inside()
    core_done(1)
    lax.fori_loop(0, blocks, compute_block, 0)
    row_done(2)
    fold(0)
    core_done(0)
    settle(per_all.at[0:outer - 1, 0], p_send.at[0], p_recv.at[0])
    for one in per_turn:
        one.start()
    wide_done(2)
    row_done(1)
    row_done(0)
    for one in per_turn:
        one.wait()
    wide_done(1)
    finish(2)
    wide_done(0)
    finish(1)
    finish(0)


def place(dirs, low, prods, elem_out, prod_out, elems, held, sems):
    slots = elems.shape[0]
    copies = []
    for slot in range(slots):
        chosen = dirs[0:1, slot:slot + 1]
        value = low[0].astype(jnp.float32)
        other = prods[0]
        for d in range(1, slots):
            value = jnp.where(chosen[None] == d, low[d].astype(jnp.float32), value)
            other = jnp.where(chosen[None] == d, prods[d], other)
        elems[slot] = value
        copies.append(pltpu.make_async_copy(elems.at[slot], elem_out.at[slot], sems.at[slot]))
        copies[-1].start()
        held[slot] = other
    copies.append(pltpu.make_async_copy(held, prod_out, sems.at[slots]))
    copies[-1].start()
    for one in copies:
        one.wait()


def on_device(vectors, links, directions, peram):
    count, _, _, planes, lanes = vectors.shape
    wides = lax.axis_size("wide")
    narrows = lax.axis_size("narrow")
    slots = directions.shape[0]
    cols = peram.shape[2]
    rows = count // wides
    share = 2 * rows // narrows
    across = narrows // 2
    norm = 1.0 / math.sqrt(12.0 * planes * wides * lanes * narrows)
    turned = vectors.transpose(3, 1, 2, 0, 4).reshape(planes, 6, count, lanes)
    vmem = pl.BlockSpec(memory_space=pltpu.VMEM)
    low = jnp.bfloat16
    dma = pltpu.SemaphoreType.DMA
    lows, prods = pl.pallas_call(
        functools.partial(kernel, wides, narrows, norm),
        out_shape=(
            jax.ShapeDtypeStruct((slots, 2, rows, count), jnp.bfloat16),
            jax.ShapeDtypeStruct((slots, 2, rows, cols), jnp.float32),
        ),
        in_specs=[vmem, vmem, vmem],
        out_specs=(vmem, vmem),
        scratch_shapes=[
            pltpu.VMEM((planes, 6, count * LZ // lanes, lanes), low),
            pltpu.VMEM((6, count, lanes), low),
            pltpu.VMEM((planes, 6, count * LZ // lanes, lanes), low),
            pltpu.VMEM((count, planes * 6 * lanes), low),
            pltpu.VMEM((count, planes * 6 * lanes), low),
            pltpu.VMEM((2, count, count), jnp.float32),
            pltpu.VMEM((3, 2, across, wides, share, count), jnp.float32),
            pltpu.VMEM((3, 2, across, wides, share, count), low),
            pltpu.VMEM((3, across, wides, share, count), low),
            pltpu.VMEM((3, across - 1, wides, share, count), low),
            pltpu.VMEM((3, wides - 1, share, count), low),
            pltpu.VMEM((3, share, count), low),
            pltpu.VMEM((3, narrows, share, count), low),
            pltpu.VMEM((rows, 2 * cols), low),
            pltpu.VMEM((wides // INNER, INNER, rows, 2 * cols), low),
            dma((count // BLOCK + 1,)), dma((count // BLOCK + 1,)),
            dma((INNER,)), dma((INNER,)),
            dma((3, 2)), dma((3, 2)),
            dma((3,)), dma((3,)),
            dma((3,)), dma((3,)),
            dma((3,)), dma((3,)),
        ],
        compiler_params=pltpu.CompilerParams(
            collective_id=0, has_side_effects=True, vmem_limit_bytes=50 * 2**20),
    )(turned, links, peram)
    anywhere = pl.BlockSpec(memory_space=pl.ANY)
    return pl.pallas_call(
        place,
        out_shape=(
            jax.ShapeDtypeStruct((slots, 2, rows, count), jnp.float32),
            jax.ShapeDtypeStruct((slots, 2, rows, cols), jnp.float32),
        ),
        in_specs=[vmem, vmem, vmem],
        out_specs=(anywhere, anywhere),
        scratch_shapes=[
            pltpu.VMEM((slots, 2, rows, count), jnp.float32),
            pltpu.VMEM((slots, 2, rows, cols), jnp.float32),
            dma((slots + 1,)),
        ],
        compiler_params=pltpu.CompilerParams(vmem_limit_bytes=8 * 2**20),
    )(directions.reshape(1, slots), lows, prods)


def solution(mesh):
    placed = (
        P("grp", None, None, "wide", "narrow"),
        P("grp", None, None, None, "wide", "narrow"),
        P(),
        P("grp", "wide", "narrow"),
    )
    return jax.shard_map(
        on_device,
        mesh=mesh,
        in_specs=placed,
        out_specs=(P("grp", None, "wide", None), P("grp", None, "wide", "narrow")),
        check_vma=False,
    )
```

```python
import functools
import math

import jax
import jax.numpy as jnp
from jax import lax
from jax.experimental import pallas as pl
from jax.experimental.pallas import tpu as pltpu
from jax.sharding import PartitionSpec as P

LZ = 16
ORDER = (2, 1, 0)
CHUNK = 32
BLOCK = 256
INNER = 2
MESH = pl.DeviceIdType.MESH
NT = (((1,), (1,)), ((), ()))


def kernel(wides, narrows, norm, vec, links, peram, low_out, prod_out,
           pack, halo0, halo1, f_re, f_im, half, keep, part, got_core, got_row, got_wide,
           thin, full, per_own, per_all,
           h_send, h_recv, p_send, p_recv, c_send, c_recv, r_send, r_recv,
           w_send, w_recv, g_send, g_recv):
    planes, comps, count, lanes = vec.shape
    groups = lanes // LZ
    per_group = count // groups
    rows = count // wides
    share = 2 * rows // narrows
    across = narrows // 2
    me_w = lax.axis_index("wide")
    me_n = lax.axis_index("narrow")
    core = lax.rem(me_n, 2)
    me_x = me_n // 2
    outer = wides // INNER
    me_z = me_w // INNER
    me_y = lax.rem(me_w, INNER)
    cols = peram.shape[2]

    def at_wide(step):
        return {"wide": lax.rem(me_w + step, wides)}

    def at_narrow(step):
        return {"narrow": lax.rem(me_n + step, narrows)}

    def at_row(step):
        return {"narrow": lax.rem(me_x + step, across) * 2 + core}

    def copy(src, dst, send, recv, where):
        return pltpu.make_async_remote_copy(
            src_ref=src, dst_ref=dst, send_sem=send, recv_sem=recv,
            device_id=where, device_id_type=MESH)

    barrier = pltpu.get_barrier_semaphore()
    for step in range(1, wides):
        pl.semaphore_signal(barrier, inc=1, device_id=at_wide(step), device_id_type=MESH)
    for step in range(1, narrows):
        pl.semaphore_signal(barrier, inc=1, device_id=at_narrow(step), device_id_type=MESH)

    lane = lax.broadcasted_iota(jnp.int32, (CHUNK, lanes), 1)

    def pack_rows(i, carry):
        slab = i // (per_group // CHUNK)
        start = pl.multiple_of(lax.rem(i, per_group // CHUNK) * CHUNK, CHUNK)
        plane = slab // comps
        comp = lax.rem(slab, comps)
        total = jnp.zeros((CHUNK, lanes), jnp.float32)
        for group in range(groups):
            piece = vec[plane, comp, pl.ds(group * per_group + start, CHUNK), :].astype(jnp.float32)
            if group:
                piece = pltpu.roll(piece, group * LZ, 1)
            total = jnp.where(lane // LZ == group, piece, total)
        pack[plane, comp, pl.ds(start, CHUNK), :] = total.astype(jnp.bfloat16)
        return carry

    pl.semaphore_wait(barrier, wides + narrows - 2)
    blocks = count // BLOCK

    def first_copy(q):
        here = pl.ds(q * BLOCK if isinstance(q, int) else pl.multiple_of(q * BLOCK, BLOCK), BLOCK)
        return copy(vec.at[0, :, here, :], halo0.at[:, here, :], h_send.at[q], h_recv.at[q],
                    at_wide(wides - 1))

    second_copy = copy(pack, halo1, h_send.at[blocks], h_recv.at[blocks], at_narrow(narrows - 1))
    for q in range(blocks):
        first_copy(q).start()
    lax.fori_loop(0, planes * comps * (per_group // CHUNK), pack_rows, 0)
    second_copy.start()
    per_own[...] = jnp.concatenate([peram[c].astype(jnp.float32) for c in range(2)], 1).astype(jnp.bfloat16)
    for step in range(1, outer):
        copy(per_own, per_all.at[me_z, me_y], p_send.at[0], p_recv.at[0],
             {"wide": lax.rem(me_z + step, outer) * INNER + me_y}).start()
    per_all[me_z, me_y] = per_own[...]
    per_turn = [
        copy(per_all.at[:, me_y], per_all.at[:, me_y], p_send.at[step], p_recv.at[step],
             {"wide": me_z * INNER + lax.rem(me_y + step, INNER)})
        for step in range(1, INNER)
    ]

    def settle(ref, send, recv):
        one = copy(ref, ref, send, recv, at_wide(1))
        one.wait_send()
        one.wait_recv()

    def shifted(direction, plane, comp, start):
        here = pl.ds(start, CHUNK)
        if direction == 0:
            if plane + 1 < planes:
                return vec[plane + 1, comp, here, :].astype(jnp.float32)
            return halo0[comp, here, :].astype(jnp.float32)
        own = vec[plane, comp, here, :].astype(jnp.float32)
        if direction == 1:
            group = start // per_group
            inside = pl.multiple_of(lax.rem(start, per_group), CHUNK)
            ahead = halo1[plane, comp, pl.ds(inside, CHUNK), :].astype(jnp.float32)
            ahead = pltpu.roll(ahead, lanes - LZ - LZ * group, 1)
            return jnp.where(lane < lanes - LZ, pltpu.roll(own, lanes - LZ, 1), ahead)
        return jnp.where(
            lax.rem(lane, LZ) < LZ - 1, pltpu.roll(own, lanes - 1, 1), pltpu.roll(own, LZ - 1, 1))

    def forward(direction, planes_here=None, first=0, past=count):
        for plane in planes_here or range(planes):
            def chunk(i, carry):
                start = pl.multiple_of(i * CHUNK, CHUNK)
                values = [shifted(direction, plane, comp, start) for comp in range(comps)]
                for a in range(3):
                    real = imag = None
                    for b in range(3):
                        link_r = links[direction, 0, a, b, plane:plane + 1, :]
                        link_i = links[direction, 1, a, b, plane:plane + 1, :]
                        term_r = link_r * values[b] - link_i * values[3 + b]
                        term_i = link_r * values[3 + b] + link_i * values[b]
                        real = term_r if real is None else real + term_r
                        imag = term_i if imag is None else imag + term_i
                    real = real.astype(jnp.bfloat16)
                    imag = imag.astype(jnp.bfloat16)
                    low = (plane * comps + a) * lanes
                    high = low + 3 * lanes
                    f_re[pl.ds(start, CHUNK), low:low + lanes] = real
                    f_re[pl.ds(start, CHUNK), high:high + lanes] = imag
                    f_im[pl.ds(start, CHUNK), low:low + lanes] = imag
                    f_im[pl.ds(start, CHUNK), high:high + lanes] = -real
                return carry

            lax.fori_loop(first // CHUNK, past // CHUNK, chunk, 0)

    inside = (planes - 1) * comps * lanes

    def columns(planes_here):
        return jnp.concatenate([vec[plane, comp] for plane in planes_here for comp in range(comps)], 1)

    def compute(direction):
        left = columns(range(planes))
        half[0] = lax.dot_general(left, f_re[...], NT, preferred_element_type=jnp.float32)
        half[1] = lax.dot_general(left, f_im[...], NT, preferred_element_type=jnp.float32)

    def compute_inside():
        left = columns(range(planes - 1))
        half[0] = lax.dot_general(left, f_re[:, :inside], NT, preferred_element_type=jnp.float32)
        half[1] = lax.dot_general(left, f_im[:, :inside], NT, preferred_element_type=jnp.float32)

    def compute_block(q, carry):
        first_copy(q).wait()
        here = pl.ds(pl.multiple_of(q * BLOCK, BLOCK), BLOCK)
        forward(0, range(planes - 1, planes), q * BLOCK, q * BLOCK + BLOCK)
        right = jnp.concatenate([f_re[here, inside:], f_im[here, inside:]], 0)
        both = lax.dot_general(
            columns(range(planes - 1, planes)), right, NT, preferred_element_type=jnp.float32)
        for c in range(2):
            half[c, :, here] = half[c, :, here] + both[:, c * BLOCK:(c + 1) * BLOCK]
        return carry

    def fold(direction):
        block = lanes
        for c in range(2):
            for top in range(0, count, block):
                turned = half[c, :, top:top + block].T
                own = half[c, top:top + block, :]
                terms = ((own - turned) if c == 0 else (own + turned)) * norm
                for low in range(0, block, share):
                    row = top + low
                    owner = c * across + (row % rows) // share
                    piece = terms[low:low + share]
                    keep[direction, owner % 2, owner // 2, row // rows] = piece
                    part[direction, owner % 2, owner // 2, row // rows] = piece.astype(jnp.bfloat16)
            core_copy(direction, c).start()

    def core_copy(d, c):
        here = pl.ds(c * (across // 2), across // 2)
        return copy(part.at[d, 1 - core, here], got_core.at[d, here], c_send.at[d, c], c_recv.at[d, c],
                    {"narrow": me_x * 2 + 1 - core})

    def row_copy(d, step):
        return copy(part.at[d, core, lax.rem(me_x + step, across)], got_row.at[d, step - 1],
                    r_send.at[d], r_recv.at[d], at_row(step))

    def wide_copy(d, step):
        return copy(part.at[d, core, me_x, lax.rem(me_w + step, wides)],
                    got_wide.at[d, step - 1],
                    w_send.at[d], w_recv.at[d], at_wide(step))

    def full_copy(d, step):
        return copy(thin.at[d], full.at[d, me_n], g_send.at[d], g_recv.at[d],
                    at_narrow(step))

    def core_done(d):
        for c in range(2):
            core_copy(d, c).wait()
        for x in range(across):
            def add(w, carry):
                total = keep[d, core, x, w] + got_core[d, x, w].astype(jnp.float32)
                keep[d, core, x, w] = total
                part[d, core, x, w] = total.astype(jnp.bfloat16)
                return carry
            lax.fori_loop(0, wides, add, 0)
        for step in range(1, across):
            row_copy(d, step).start()

    def row_done(d):
        settle(got_row.at[d], r_send.at[d], r_recv.at[d])

        def add(w, carry):
            total = keep[d, core, me_x, w]
            for step in range(1, across):
                total = total + got_row[d, step - 1, w].astype(jnp.float32)
            keep[d, core, me_x, w] = total
            part[d, core, me_x, w] = total.astype(jnp.bfloat16)
            return carry

        lax.fori_loop(0, wides, add, 0)
        for step in range(1, wides):
            wide_copy(d, step).start()

    def wide_wait(d):
        settle(got_wide.at[d], w_send.at[d], w_recv.at[d])

    def wide_done(d, waited=False):
        if not waited:
            wide_wait(d)
        total = keep[d, core, me_x, me_w]
        for step in range(1, wides):
            total = total + got_wide[d, step - 1].astype(jnp.float32)
        total = total.astype(jnp.bfloat16)
        thin[d] = total
        full[d, me_n] = total
        for step in range(1, narrows):
            full_copy(d, step).start()

    def finish(d):
        settle(full.at[d, 0:narrows - 1], g_send.at[d], g_recv.at[d])
        real = full[d, 0:across].astype(jnp.float32).reshape(rows, count).astype(jnp.bfloat16)
        imag = full[d, across:narrows].astype(jnp.float32).reshape(rows, count).astype(jnp.bfloat16)
        low_out[d, 0] = real
        low_out[d, 1] = imag
        both = per_all[...].astype(jnp.float32).reshape(count, 2 * cols).astype(jnp.bfloat16)

        def times(x):
            return jnp.dot(x, both, preferred_element_type=jnp.float32)

        first = times(real)
        second = times(imag)
        prod_out[d, 0] = first[:, :cols] - second[:, cols:]
        prod_out[d, 1] = first[:, cols:] + second[:, :cols]

    forward(2)
    compute(2)
    fold(2)
    second_copy.wait()
    forward(1)
    core_done(2)
    compute(1)
    fold(1)
    forward(0, range(planes - 1))
    compute_inside()
    core_done(1)
    lax.fori_loop(0, blocks, compute_block, 0)
    row_done(2)
    fold(0)
    core_done(0)
    settle(per_all.at[0:outer - 1, 0], p_send.at[0], p_recv.at[0])
    for one in per_turn:
        one.start()
    wide_wait(2)
    row_done(1)
    row_done(0)
    wide_done(2, True)
    for one in per_turn:
        one.wait()
    wide_done(1)
    wide_done(0)
    finish(2)
    finish(1)
    finish(0)


def place(dirs, low, prods, elem_out, prod_out, elems, held, sems):
    slots = elems.shape[0]
    copies = []
    for slot in range(slots):
        chosen = dirs[0:1, slot:slot + 1]
        value = low[0].astype(jnp.float32)
        other = prods[0]
        for d in range(1, slots):
            value = jnp.where(chosen[None] == d, low[d].astype(jnp.float32), value)
            other = jnp.where(chosen[None] == d, prods[d], other)
        elems[slot] = value
        copies.append(pltpu.make_async_copy(elems.at[slot], elem_out.at[slot], sems.at[slot]))
        copies[-1].start()
        held[slot] = other
    copies.append(pltpu.make_async_copy(held, prod_out, sems.at[slots]))
    copies[-1].start()
    for one in copies:
        one.wait()


def on_device(vectors, links, directions, peram):
    count, _, _, planes, lanes = vectors.shape
    wides = lax.axis_size("wide")
    narrows = lax.axis_size("narrow")
    slots = directions.shape[0]
    cols = peram.shape[2]
    rows = count // wides
    share = 2 * rows // narrows
    across = narrows // 2
    norm = 1.0 / math.sqrt(12.0 * planes * wides * lanes * narrows)
    turned = vectors.transpose(3, 1, 2, 0, 4).reshape(planes, 6, count, lanes)
    vmem = pl.BlockSpec(memory_space=pltpu.VMEM)
    low = jnp.bfloat16
    dma = pltpu.SemaphoreType.DMA
    lows, prods = pl.pallas_call(
        functools.partial(kernel, wides, narrows, norm),
        out_shape=(
            jax.ShapeDtypeStruct((slots, 2, rows, count), jnp.bfloat16),
            jax.ShapeDtypeStruct((slots, 2, rows, cols), jnp.float32),
        ),
        in_specs=[vmem, vmem, vmem],
        out_specs=(vmem, vmem),
        scratch_shapes=[
            pltpu.VMEM((planes, 6, count * LZ // lanes, lanes), low),
            pltpu.VMEM((6, count, lanes), low),
            pltpu.VMEM((planes, 6, count * LZ // lanes, lanes), low),
            pltpu.VMEM((count, planes * 6 * lanes), low),
            pltpu.VMEM((count, planes * 6 * lanes), low),
            pltpu.VMEM((2, count, count), jnp.float32),
            pltpu.VMEM((3, 2, across, wides, share, count), jnp.float32),
            pltpu.VMEM((3, 2, across, wides, share, count), low),
            pltpu.VMEM((3, across, wides, share, count), low),
            pltpu.VMEM((3, across - 1, wides, share, count), low),
            pltpu.VMEM((3, wides - 1, share, count), low),
            pltpu.VMEM((3, share, count), low),
            pltpu.VMEM((3, narrows, share, count), low),
            pltpu.VMEM((rows, 2 * cols), low),
            pltpu.VMEM((wides // INNER, INNER, rows, 2 * cols), low),
            dma((count // BLOCK + 1,)), dma((count // BLOCK + 1,)),
            dma((INNER,)), dma((INNER,)),
            dma((3, 2)), dma((3, 2)),
            dma((3,)), dma((3,)),
            dma((3,)), dma((3,)),
            dma((3,)), dma((3,)),
        ],
        compiler_params=pltpu.CompilerParams(
            collective_id=0, has_side_effects=True, vmem_limit_bytes=50 * 2**20),
    )(turned, links, peram)
    anywhere = pl.BlockSpec(memory_space=pl.ANY)
    return pl.pallas_call(
        place,
        out_shape=(
            jax.ShapeDtypeStruct((slots, 2, rows, count), jnp.float32),
            jax.ShapeDtypeStruct((slots, 2, rows, cols), jnp.float32),
        ),
        in_specs=[vmem, vmem, vmem],
        out_specs=(anywhere, anywhere),
        scratch_shapes=[
            pltpu.VMEM((slots, 2, rows, count), jnp.float32),
            pltpu.VMEM((slots, 2, rows, cols), jnp.float32),
            dma((slots + 1,)),
        ],
        compiler_params=pltpu.CompilerParams(vmem_limit_bytes=8 * 2**20),
    )(directions.reshape(1, slots), lows, prods)


def solution(mesh):
    placed = (
        P("grp", None, None, "wide", "narrow"),
        P("grp", None, None, None, "wide", "narrow"),
        P(),
        P("grp", "wide", "narrow"),
    )
    return jax.shard_map(
        on_device,
        mesh=mesh,
        in_specs=placed,
        out_specs=(P("grp", None, "wide", None), P("grp", None, "wide", "narrow")),
        check_vma=False,
    )
```
